768 devices in a mesh: segment: 24 (over z, core), expert: 32 (over y, x).
Axes of the slice: x: 4, y: 8, z: 12, core: 2. Of those that a mesh axis runs over, the one named last changes fastest.
Arguments:
- hidden: bfloat16 [24, 2048, 4096], P('segment', 'expert'), may hold values from -6 to 6
- expert_ids: int32 [2, 24, 2048, 8], P(None, 'segment', 'expert'), may hold values from 0 to 127, as said below
- route_weights: float32 [2, 24, 2048, 8], P(None, 'segment', 'expert'), may hold values from 0.2 to 1
- norm_gain: bfloat16 [24, 4096], P('segment'), may hold values from 0.099609375 to 1.8984375
- w_gate: bfloat16 [24, 4096, 4096], P('segment', None, 'expert'), may hold values from -0.09375 to 0.09375
- w_up: bfloat16 [24, 4096, 4096], P('segment', None, 'expert'), may hold values from -0.09375 to 0.09375
- w_down: bfloat16 [24, 4096, 4096], P('segment', 'expert'), may hold values from -0.1875 to 0.1875
Outputs:
- handed: bfloat16 [24, 2048, 4096], P('segment', 'expert')
The draws below stay inside these ranges and needn't reach their ends.
Inputs may be any that keep to these rules, and one draw needn't show every extreme that they name: `expert_ids`: each row names 8 different experts. In each aligned block of 64 rows (the rows of one device) each of the experts 0 .. 3 is named by at most 8 rows, and some expert of them by exactly 8 rows in every block.
All inputs are finite; a program needn't handle non-finite values.
Results may differ from the reference program's by a relative error of at most 0.0034.
Values may be sent and summed in bfloat16 or wider, within the bound.
A program may use at most 32 MiB of HBM per device.

```python
import jax
import jax.numpy as jnp
from jax import lax

D = 4096
FF = 1024
EXPERTS = 128
TOP = 8
SLICES = 8
MOST = 8
TICKS = 2
TOK_DEV = 64
SEGMENTS = 24
ROWS = 2048
WIN_EXPERTS = 4


def draw_expert_ids(key, part):
    block_count = TICKS * SEGMENTS * (ROWS // TOK_DEV)
    key_list = jax.random.split(jax.random.fold_in(key, 17), 7)
    window_ids = jnp.arange(WIN_EXPERTS, dtype=jnp.int32)
    ceiling = jax.random.randint(key_list[0], (WIN_EXPERTS,), 1, MOST + 1)
    full_expert = jax.random.randint(key_list[1], (), 0, WIN_EXPERTS)
    loads = jnp.minimum(jax.random.randint(key_list[2], (block_count, WIN_EXPERTS), 0, MOST + 1), ceiling[None, :])
    busy_expert = jax.random.randint(key_list[3], (block_count, 1), 0, WIN_EXPERTS)
    loads = jnp.where((window_ids[None, :] == busy_expert) | (window_ids[None, :] == full_expert), MOST, loads)
    scores = jax.random.randint(key_list[4], (block_count, WIN_EXPERTS, TOK_DEV), 0, 1048576) * TOK_DEV + jnp.arange(TOK_DEV, dtype=jnp.int32)
    row_rank = jnp.argsort(jnp.argsort(scores, axis=-1, stable=True), axis=-1, stable=True)
    members = jnp.transpose(row_rank < loads[:, :, None], (0, 2, 1))
    tie_break = jax.random.randint(key_list[5], (block_count, TOK_DEV, EXPERTS), 0, 1048576) * EXPERTS + jnp.arange(EXPERTS, dtype=jnp.int32)
    order_rank = jnp.argsort(jnp.argsort(tie_break, axis=-1, stable=True), axis=-1, stable=True)
    in_window = jnp.arange(EXPERTS, dtype=jnp.int32) < WIN_EXPERTS
    window_pad = jnp.concatenate([members, jnp.zeros((block_count, TOK_DEV, EXPERTS - WIN_EXPERTS), dtype=bool)], axis=-1)
    sort_key = jnp.where(window_pad, order_rank, jnp.where(in_window, 3 * EXPERTS + order_rank, EXPERTS + order_rank))
    chosen = jnp.argsort(sort_key, axis=-1, stable=True)[..., :TOP]
    slot_scores = jax.random.randint(key_list[6], (block_count, TOK_DEV, TOP), 0, 1048576) * TOP + jnp.arange(TOP, dtype=jnp.int32)
    slot_order = jnp.argsort(slot_scores, axis=-1, stable=True)
    routing = jnp.take_along_axis(chosen, slot_order, axis=-1)
    return routing.reshape(TICKS, SEGMENTS, ROWS, TOP).astype(jnp.int32)


def levels(stream_key, extent, shards, low, high):
    loudness = 1.0
    for position, parts in shards:
        steps = jax.random.uniform(jax.random.fold_in(jax.random.fold_in(stream_key, 6), position), (parts,), jnp.float32, low / len(shards), high / len(shards))
        loudness = loudness * jnp.repeat(jnp.exp(steps), extent[position] // parts).reshape((-1,) + (1,) * (len(extent) - 1 - position))
    return loudness


def gaussian(stream_key, dims, spread, bound, shards=(), held_as=jnp.bfloat16):
    array = spread * jax.random.normal(stream_key, dims, jnp.float32)
    if shards:
        array = array * levels(stream_key, dims, shards, -0.22, 0.18)
    return jnp.clip(array, -bound, bound).astype(held_as)


def setup_inputs(seed: int = 0) -> dict:
    seeds = jax.random.split(jax.random.key(seed), 8)
    return {
        "hidden": gaussian(seeds[0], (SEGMENTS, ROWS, D), 1.0, 6.0, ((0, 24), (1, 32))),
        "expert_ids": draw_expert_ids(jax.random.fold_in(seeds[7], 71), 0),
        "route_weights": jnp.clip(0.2 + 0.8 * jax.random.uniform(seeds[2], (TICKS, SEGMENTS, ROWS, TOP), jnp.float32) ** levels(seeds[2], (TICKS, SEGMENTS, ROWS, TOP), ((1, 24), (2, 32)), -0.2, 0.2), 0.2, 1.0),
        "norm_gain": jnp.clip(1.0 + 0.18 * jax.random.normal(seeds[3], (SEGMENTS, D), jnp.float32), 0.099609375, 1.8984375).astype(jnp.bfloat16),
        "w_gate": gaussian(seeds[4], (SEGMENTS, D, WIN_EXPERTS * FF), D ** -0.5, 0.09375, ((0, 24), (2, 32))),
        "w_up": gaussian(seeds[5], (SEGMENTS, D, WIN_EXPERTS * FF), D ** -0.5, 0.09375, ((0, 24), (2, 32))),
        "w_down": gaussian(seeds[6], (SEGMENTS, WIN_EXPERTS * FF, D), FF ** -0.5, 0.1875, ((0, 24), (1, 32))),
    }


EPS = 1e-06

def segment_layer(current, route_ids, route_weight, gain_row, w_gate, w_up, w_down):
    widened = current.astype(jnp.float32)
    normed = (widened * lax.rsqrt(lax.optimization_barrier(jnp.mean(widened * widened, axis=-1, keepdims=True)) + EPS) * gain_row.astype(jnp.float32)).astype(jnp.bfloat16)
    matches = route_ids[:, :, None] == jnp.arange(WIN_EXPERTS, dtype=jnp.int32)[None, None, :]
    members = jnp.any(matches, axis=1)
    route_share = lax.optimization_barrier(jnp.sum(jnp.where(matches, route_weight[:, :, None], jnp.float32(0.0)), axis=1))
    slot_limit = ROWS // TOK_DEV * MOST
    slice_width = FF // SLICES
    branch = jnp.zeros((ROWS, D), jnp.float32)
    for expert_index in range(WIN_EXPERTS):
        picked = jnp.nonzero(members[:, expert_index], size=slot_limit, fill_value=0)[0].astype(jnp.int32)
        row_count = jnp.sum(members[:, expert_index].astype(jnp.int32))
        in_range = jnp.arange(slot_limit, dtype=jnp.int32) < row_count
        taken_rows = normed[picked]
        column_start = expert_index * FF
        gate_out = jnp.dot(taken_rows, w_gate[:, column_start:column_start + FF], preferred_element_type=jnp.float32)
        up_out = jnp.dot(taken_rows, w_up[:, column_start:column_start + FF], preferred_element_type=jnp.float32)
        active = (jax.nn.silu(gate_out) * up_out).astype(jnp.bfloat16)
        slice_sum = jnp.zeros((slot_limit, D), jnp.float32)
        for slice_index in range(SLICES):
            row_start = column_start + slice_index * slice_width
            slice_out = jnp.dot(active[:, slice_index * slice_width:(slice_index + 1) * slice_width], w_down[row_start:row_start + slice_width], preferred_element_type=jnp.float32)
            slice_sum = slice_sum + lax.optimization_barrier(slice_out.astype(jnp.bfloat16)).astype(jnp.float32)
        weighted = jnp.where(in_range, route_share[picked, expert_index], jnp.float32(0.0))
        branch = branch.at[picked].add(weighted[:, None] * slice_sum)
    return (widened + branch).astype(jnp.bfloat16)

def apply_layer(segment_args):
    return segment_layer(*segment_args)

def reference(hidden, expert_ids, route_weights, norm_gain, w_gate, w_up, w_down):
    current = hidden
    for tick_index in range(TICKS):
        finished = lax.map(apply_layer, (current, expert_ids[tick_index], route_weights[tick_index], norm_gain, w_gate, w_up, w_down))
        current = jnp.roll(finished, 1, axis=0)
    return current
```

```python
import functools

import jax
import jax.numpy as jnp
from jax import lax
from jax.experimental import pallas as pl
from jax.experimental.pallas import tpu as pltpu
from jax.sharding import PartitionSpec as P

EPS = 1e-06
TICKS = 2
PAIRS = 4
GROUP = 8
XS = 4
CAP = 8
ORDER = (0, 1, 3, 2)
MESH = pl.DeviceIdType.MESH
F32 = jnp.float32
BF16 = jnp.bfloat16


def kernel(
    hid, ids, rw, gain, wg, wu, wd, out,
    xin, ids_v, rw_v, gain_v, wgu, wd2, xcur, xprev, wloc, wprev, place, packed, rbuf, act, outb, ret,
    loc_sem, wd_send, wd_recv, y_send, y_recv, xf_send, xf_recv, xh_send, xh_recv,
    act_send, act_recv, ret_send, ret_recv, nx_send, nx_recv, nw_send, nw_recv,
):
    segments = lax.axis_size("segment")
    rows, width = xcur.shape
    half = width // 2
    cols = width // GROUP
    s = lax.axis_index("segment")
    p = lax.axis_index("expert")
    pr = p // GROUP
    q = p % GROUP
    b = q // XS
    x = q % XS
    nxt = lax.rem(s + 1, segments)
    prv = lax.rem(s + segments - 1, segments)
    right = lax.rem(x + 1, XS)
    left = lax.rem(x + XS - 1, XS)
    mate = 1 - b

    barrier = pltpu.get_barrier_semaphore()

    def greet(seg, exp):
        pl.semaphore_signal(barrier, inc=1, device_id=(seg, exp), device_id_type=MESH)

    for step in range(1, GROUP):
        greet(s, pr * GROUP + lax.rem(q + step, GROUP))
    for step in range(1, PAIRS):
        for row in range(2):
            greet(s, lax.rem(pr + step, PAIRS) * GROUP + row * XS + x)
    for owner in range(PAIRS * GROUP):
        greet(prv, owner)
    count = GROUP - 1 + 2 * (PAIRS - 1) + PAIRS * GROUP

    loads = [
        (hid.at[0], xin),
        (ids.at[:, 0], ids_v),
        (rw.at[:, 0], rw_v),
        (gain, gain_v),
        (wg.at[0], wgu.at[:, 0:128]),
        (wu.at[0], wgu.at[:, 128:256]),
        (wd.at[0, :, pl.ds(pl.multiple_of(q * cols, 128), cols)], wd2.at[q]),
    ]
    copies = [pltpu.make_async_copy(a, c, loc_sem.at[i]) for i, (a, c) in enumerate(loads)]
    for c in copies:
        c.start()

    def remote(src, dst, send, recv, seg, exp):
        return pltpu.make_async_remote_copy(
            src_ref=src, dst_ref=dst, send_sem=send, recv_sem=recv, device_id=(seg, exp), device_id_type=MESH
        )

    copies[1].wait()
    copies[2].wait()
    lane = lax.broadcasted_iota(jnp.int32, (rows, 128), 1)
    lane_e = lax.rem(lane, 32) // CAP
    lane_c = lax.rem(lane, CAP)
    tri = (
        lax.broadcasted_iota(jnp.int32, (rows, rows), 0) >= lax.broadcasted_iota(jnp.int32, (rows, rows), 1)
    ).astype(F32).astype(BF16)
    for t in range(TICKS):
        share = jnp.zeros((rows, 128), F32)
        member = jnp.zeros((rows, 128), F32)
        idt = ids_v[t]
        rwt = rw_v[t]
        for k in range(idt.shape[1]):
            hit = idt[:, k : k + 1] == lane_e
            share = share + jnp.where(hit, rwt[:, k : k + 1], F32(0.0))
            member = jnp.where(hit, F32(1.0), member)
        rank = jnp.dot(tri, member.astype(BF16), preferred_element_type=F32)
        placed = jnp.where(rank == (lane_c + 1).astype(F32), member, F32(0.0))
        place[t] = placed.astype(BF16)
        weight = placed * share
        high = weight.astype(BF16)
        low = (weight - high.astype(F32)).astype(BF16)
        zero = jnp.zeros_like(weight)
        wloc[t] = jnp.where(lane < 32, high.astype(F32), jnp.where(lane < 64, low.astype(F32), zero)).astype(BF16)

    copies[0].wait()
    copies[3].wait()

    def norm_pack(t, source):
        total = jnp.zeros((rows, 1), F32)
        for j in range(GROUP):
            v = source[:, j * cols : (j + 1) * cols].astype(F32)
            total = total + jnp.sum(v * v, axis=-1, keepdims=True)
        scale = lax.rsqrt(total / width + EPS)
        pick = place[t][:, 0:32]
        for j in range(GROUP):
            v = source[:, j * cols : (j + 1) * cols].astype(F32)
            g = gain_v[0:1, j * cols : (j + 1) * cols].astype(F32)
            normed = (v * scale * g).astype(BF16)
            rowset = lax.dot_general(pick, normed, (((0,), (0,)), ((), ())), preferred_element_type=F32)
            packed[t, :, :, j * cols : (j + 1) * cols] = rowset.astype(BF16).reshape(PAIRS, CAP, cols)

    norm_pack(0, xin)
    pl.semaphore_wait(barrier, count)

    def combine(t, target):
        remote(xprev.at[t], xprev.at[t], nx_send.at[t], nx_recv.at[t], nxt, p).wait_recv()
        remote(wprev.at[t], wprev.at[t], nw_send.at[t], nw_recv.at[t], nxt, p).wait_recv()
        remote(ret.at[t], ret.at[t], ret_send.at[t], ret_recv.at[t], nxt, p).wait_recv()
        w = wprev[t][:, 0:64]
        for j in range(GROUP):
            r = ret[t, :, j].reshape(PAIRS * CAP, cols)
            rr = jnp.concatenate([r, r], axis=0)
            branch = jnp.dot(w, rr, preferred_element_type=F32)
            target(j, xprev[t, :, j * cols : (j + 1) * cols].astype(F32) + branch)

    for t in range(TICKS):
        if t > 0:
            def keep(j, v):
                xcur[:, j * cols : (j + 1) * cols] = v.astype(BF16)

            combine(t - 1, keep)
            norm_pack(t, xcur)
        for d in range(PAIRS):
            dest = lax.rem(pr + PAIRS - ORDER[d], PAIRS)
            targets = [mate] if d == 0 else ([0, 1] if d != 1 else [1, 0])
            for row in targets:
                remote(
                    packed.at[t, dest], rbuf.at[t, pr, q], y_send.at[t], y_recv.at[t * 8 + d * 2 + b],
                    s, dest * GROUP + row * XS + x,
                ).start()
        rbuf[t, pr, q] = packed[t, pr]
        remote(hid.at[0] if t == 0 else xcur, xprev.at[t], nx_send.at[t], nx_recv.at[t], nxt, p).start()
        remote(wloc.at[t], wprev.at[t], nw_send.at[t], nw_recv.at[t], nxt, p).start()

        def block_of(k):
            d, i = k // 2, k % 2
            pp = lax.rem(pr + ORDER[d], PAIRS)
            if d == 0:
                row = b if i == 0 else mate
            elif d == 1:
                row = i
            else:
                row = 1 - i
            return d, pp, row

        def relay(k):
            d, pp, row = block_of(k)
            from_left = rbuf.at[t, pp, row * XS + left]
            from_right = rbuf.at[t, pp, row * XS + right]
            base = pr * GROUP + b * XS
            remote(from_left, from_left, xf_send.at[t], xf_recv.at[t, k, 0], s, base + right).wait_recv()
            part = from_left.at[:, 0:half]
            remote(part, part, xh_send.at[t], xh_recv.at[t, k, 0], s, base + right).start()
            remote(from_right, from_right, xf_send.at[t], xf_recv.at[t, k, 1], s, base + left).wait_recv()
            part = from_right.at[:, half:width]
            remote(part, part, xh_send.at[t], xh_recv.at[t, k, 1], s, base + left).start()

        def gate_up(d):
            base = pr * GROUP + b * XS
            for k in (2 * d, 2 * d + 1):
                _, pp, row = block_of(k)
                far = rbuf.at[t, pp, row * XS + lax.rem(x + 2, XS)]
                for side, span in ((0, (0, half)), (1, (half, width))):
                    part = far.at[:, span[0] : span[1]]
                    remote(part, part, xh_send.at[t], xh_recv.at[t, k, side], s, base + right).wait_recv()
            pp = lax.rem(pr + ORDER[d], PAIRS)
            taken = rbuf[t, pp].reshape(GROUP * CAP, width)
            both = jnp.dot(taken, wgu[...], preferred_element_type=F32)
            gate, up = both[:, 0:128], both[:, 128:256]
            act[t, q, pp] = (gate / (1.0 + jnp.exp(-gate)) * up).astype(BF16)
            for step in range(1, GROUP):
                other = lax.rem(q + step, GROUP)
                remote(
                    act.at[t, q, pp], act.at[t, q, pp], act_send.at[t], act_recv.at[t, d], s, pr * GROUP + other
                ).start()

        for k in range(2 * PAIRS):
            d, pp, row = block_of(k)
            mine = rbuf.at[t, pp, row * XS + x]
            base = pr * GROUP + b * XS
            if k > 0:
                remote(mine, mine, y_send.at[t], y_recv.at[t * 8 + d * 2 + row], s, base + right).wait_recv()
            remote(mine, mine, xf_send.at[t], xf_recv.at[t, k, 0], s, base + right).start()
            remote(mine, mine, xf_send.at[t], xf_recv.at[t, k, 1], s, base + left).start()
            if t == 0 and k > 0:
                other = lax.rem(q + k, GROUP)
                remote(
                    wd.at[0, :, pl.ds(pl.multiple_of(other * cols, 128), cols)], wd2.at[q],
                    wd_send.at[0], wd_recv.at[0], s, pr * GROUP + other,
                ).start()
            if k > 0:
                relay(k - 1)
            if t == 0 and k == 3:
                copies[4].wait()
                copies[5].wait()
            if k % 2 == 1 and k > 1:
                gate_up((k - 3) // 2)
        relay(2 * PAIRS - 1)
        gate_up(PAIRS - 1)

        if t == 0:
            copies[6].wait()
            remote(wd2.at[0:7], wd2.at[0:7], wd_send.at[0], wd_recv.at[0], s, pr * GROUP).wait_recv()
        for d in range(PAIRS):
            remote(act.at[t, 0:7, 0], act.at[t, 0:7, 0], act_send.at[t], act_recv.at[t, d], s, pr * GROUP).wait_recv()
        units = jnp.concatenate([act[t, k].reshape(PAIRS * GROUP * CAP, 128) for k in range(GROUP)], axis=1)
        full = jnp.dot(units, wd2[...].reshape(GROUP * 128, cols), preferred_element_type=F32)
        outb[t] = full.astype(BF16).reshape(PAIRS * GROUP, CAP, cols)
        for step in range(PAIRS * GROUP):
            owner = lax.rem(p + step, PAIRS * GROUP)
            remote(outb.at[t, owner], ret.at[t, pr, q], ret_send.at[t], ret_recv.at[t], nxt, owner).start()

    def emit(j, v):
        out[0, :, j * cols : (j + 1) * cols] = v.astype(BF16)

    combine(TICKS - 1, emit)

    for t in range(TICKS):
        remote(rbuf.at[t, 0, 0:7], rbuf.at[t, 0, 0:7], y_send.at[t], y_recv.at[0], s, p).wait_send()
        remote(rbuf.at[t, 0:2], rbuf.at[t, 0:2], xf_send.at[t], xf_recv.at[t, 0, 0], s, p).wait_send()
        remote(rbuf.at[t, 0], rbuf.at[t, 0], xh_send.at[t], xh_recv.at[t, 0, 0], s, p).wait_send()
        remote(act.at[t, 0:7], act.at[t, 0:7], act_send.at[t], act_recv.at[t, 0], s, p).wait_send()
        remote(ret.at[t], ret.at[t], ret_send.at[t], ret_recv.at[t], s, p).wait_send()
        remote(xprev.at[t], xprev.at[t], nx_send.at[t], nx_recv.at[t], s, p).wait_send()
        remote(wprev.at[t], wprev.at[t], nw_send.at[t], nw_recv.at[t], s, p).wait_send()
    remote(wd2.at[0:7], wd2.at[0:7], wd_send.at[0], wd_recv.at[0], s, p).wait_send()


def body(hidden, expert_ids, route_weights, norm_gain, w_gate, w_up, w_down):
    _, rows, width = hidden.shape
    cols = width // GROUP
    top = expert_ids.shape[-1]
    dma = pltpu.SemaphoreType.DMA
    return pl.pallas_call(
        kernel,
        out_shape=jax.ShapeDtypeStruct(hidden.shape, BF16),
        in_specs=[pl.BlockSpec(memory_space=pl.ANY)] * 7,
        out_specs=pl.BlockSpec(memory_space=pltpu.VMEM),
        scratch_shapes=[
            pltpu.VMEM((rows, width), BF16),
            pltpu.VMEM((TICKS, rows, top), jnp.int32),
            pltpu.VMEM((TICKS, rows, top), F32),
            pltpu.VMEM((1, width), BF16),
            pltpu.VMEM((width, 256), BF16),
            pltpu.VMEM((GROUP, 128, cols), BF16),
            pltpu.VMEM((rows, width), BF16),
            pltpu.VMEM((TICKS, rows, width), BF16),
            pltpu.VMEM((TICKS, rows, 128), BF16),
            pltpu.VMEM((TICKS, rows, 128), BF16),
            pltpu.VMEM((TICKS, rows, 128), BF16),
            pltpu.VMEM((TICKS, PAIRS, CAP, width), BF16),
            pltpu.VMEM((TICKS, PAIRS, GROUP, CAP, width), BF16),
            pltpu.VMEM((TICKS, GROUP, PAIRS, GROUP * CAP, 128), BF16),
            pltpu.VMEM((TICKS, PAIRS * GROUP, CAP, cols), BF16),
            pltpu.VMEM((TICKS, PAIRS, GROUP, CAP, cols), BF16),
            dma((7,)),
            dma((1,)), dma((1,)),
            dma((TICKS,)), dma((TICKS * 8,)),
            dma((TICKS,)), dma((TICKS, 8, 2)),
            dma((TICKS,)), dma((TICKS, 8, 2)),
            dma((TICKS,)), dma((TICKS, PAIRS)),
            dma((TICKS,)), dma((TICKS,)),
            dma((TICKS,)), dma((TICKS,)),
            dma((TICKS,)), dma((TICKS,)),
        ],
        compiler_params=pltpu.CompilerParams(collective_id=0, has_side_effects=True),
    )(hidden, expert_ids, route_weights, norm_gain, w_gate, w_up, w_down)


def solution(mesh):
    return jax.shard_map(
        body,
        mesh=mesh,
        in_specs=(
            P("segment", "expert", None),
            P(None, "segment", "expert", None),
            P(None, "segment", "expert", None),
            P("segment", None),
            P("segment", None, "expert"),
            P("segment", None, "expert"),
            P("segment", "expert", None),
        ),
        out_specs=P("segment", "expert", None),
        check_vma=False,
    )
```

```python
import functools

import jax
import jax.numpy as jnp
from jax import lax
from jax.experimental import pallas as pl
from jax.experimental.pallas import tpu as pltpu
from jax.sharding import PartitionSpec as P

EPS = 1e-06
TICKS = 2
PAIRS = 4
GROUP = 8
XS = 4
CAP = 8
MESH = pl.DeviceIdType.MESH
F32 = jnp.float32
BF16 = jnp.bfloat16

def combined(x, w, r):
    r = r.reshape(PAIRS * CAP, r.shape[-1])
    branch = jnp.dot(w[:, 0:64], jnp.concatenate([r, r], axis=0), preferred_element_type=F32)
    return (x.astype(F32) + branch).astype(BF16)


def finish(x_ref, w_ref, r_ref, o_ref):
    step = 512
    for j in range(x_ref.shape[1] // step):
        span = slice(j * step, (j + 1) * step)
        o_ref[0, :, span] = combined(x_ref[:, span], w_ref[...], r_ref[:, :, span])


NEAR = (0, 1, -1, -2, 2, -3, 3, 4)
CHUNKS = ((0, 1), (2, 3), (4, 6), (5, 7))
STEPS_OUT = ((1, 1), (-1, -1), (2, -2), (-3, -3))
PLAN = (
    ("S0", "W+1", "W-1", "S1", "S2", "Wm", "R0", "S3", "R1", "S4", "W+5", "W-5", "R2", "S5", "R3", "G0", "S6", "R4", "W2", "S7", "R5", "G1", "R6", "R7", "W6", "G2", "G3", "V", "D0", "D1", "D2", "D3"),
    ("S0", "S1", "S2", "R0", "S3", "R1", "S4", "R2", "S5", "R3", "G0", "S6", "R4", "S7", "R5", "G1", "R6", "R7", "G2", "D0", "G3", "D1", "D2", "D3"),
)


def kernel(
    hid, ids, rw, gain, wg, wu, wd, x_out, w_out, r_out,
    xin, ids_v, rw_v, gain_v, wgu, wd2, xcur, xprev, wloc, wprev, place, packed, rbuf, act, outb, ret,
    loc_sem, wd_send, wd_recv, y_send, y_recv, xf_send, xf_recv, xh_send, xh_recv,
    act_send, act_recv, ret_send, ret_recv, nx_send, nx_recv, nw_send, nw_recv,
):
    segments = lax.axis_size("segment")
    rows, width = xcur.shape
    half = width // 2
    cols = width // GROUP
    s = lax.axis_index("segment")
    p = lax.axis_index("expert")
    pr = p // GROUP
    q = p % GROUP
    b = q // XS
    x = q % XS
    y = p // XS
    nxt = lax.rem(s + 1, segments)
    prv = lax.rem(s + segments - 1, segments)
    right = lax.rem(x + 1, XS)
    left = lax.rem(x + XS - 1, XS)
    across = lax.rem(x + 2, XS)
    home = y * XS
    sign = 1 - 2 * b

    def row_of(offset):
        return lax.rem(y + sign * offset + 16, 8)

    loads = [
        (ids.at[:, 0], ids_v),
        (rw.at[:, 0], rw_v),
        (hid.at[0], xin),
        (gain, gain_v),
        (wg.at[0], wgu.at[:, 0:128]),
        (wu.at[0], wgu.at[:, 128:256]),
        (wd.at[0, :, pl.ds(pl.multiple_of(q * cols, 128), cols)], wd2.at[q]),
    ]
    copies = [pltpu.make_async_copy(a, c, loc_sem.at[i]) for i, (a, c) in enumerate(loads)]
    for c in copies[:4]:
        c.start()

    barrier = pltpu.get_barrier_semaphore()

    def greet(seg, exp):
        pl.semaphore_signal(barrier, inc=1, device_id=(seg, exp), device_id_type=MESH)

    greet(prv, p)
    for step in range(1, GROUP):
        greet(s, pr * GROUP + lax.rem(q + step, GROUP))
    for offset in (-1, -2, -3):
        greet(s, row_of(offset) * XS + x)
    count = 1 + GROUP - 1 + 3
    for c in copies[4:]:
        c.start()

    def remote(src, dst, send, recv, seg, exp):
        return pltpu.make_async_remote_copy(
            src_ref=src, dst_ref=dst, send_sem=send, recv_sem=recv, device_id=(seg, exp), device_id_type=MESH
        )

    copies[0].wait()
    copies[1].wait()
    lane = lax.broadcasted_iota(jnp.int32, (rows, 128), 1)
    lane_e = lax.rem(lane, 32) // CAP
    lane_c = lax.rem(lane, CAP)
    tri = (
        lax.broadcasted_iota(jnp.int32, (rows, rows), 0) >= lax.broadcasted_iota(jnp.int32, (rows, rows), 1)
    ).astype(F32).astype(BF16)
    for t in range(TICKS):
        share = jnp.zeros((rows, 128), F32)
        member = jnp.zeros((rows, 128), F32)
        idt = jnp.transpose(ids_v[t])
        rwt = jnp.transpose(rw_v[t])
        for k in range(idt.shape[1]):
            hit = idt[:, k : k + 1] == lane_e
            share = share + jnp.where(hit, rwt[:, k : k + 1], F32(0.0))
            member = jnp.where(hit, F32(1.0), member)
        rank = jnp.dot(tri, member.astype(BF16), preferred_element_type=F32)
        placed = jnp.where(rank == (lane_c + 1).astype(F32), member, F32(0.0))
        place[t] = placed.astype(BF16)
        weight = placed * share
        high = weight.astype(BF16)
        low = (weight - high.astype(F32)).astype(BF16)
        zero = jnp.zeros_like(weight)
        wloc[t] = jnp.where(lane < 32, high.astype(F32), jnp.where(lane < 64, low.astype(F32), zero)).astype(BF16)

    def norm_pack(t, source):
        total = jnp.zeros((rows, 1), F32)
        for j in range(GROUP):
            v = source[:, j * cols : (j + 1) * cols].astype(F32)
            total = total + jnp.sum(v * v, axis=-1, keepdims=True)
        scale = lax.rsqrt(total / width + EPS)
        pick = place[t][:, 0:32]
        for j in range(GROUP):
            v = source[:, j * cols : (j + 1) * cols].astype(F32)
            g = gain_v[0:1, j * cols : (j + 1) * cols].astype(F32)
            normed = (v * scale * g).astype(BF16)
            rowset = lax.dot_general(pick, normed, (((0,), (0,)), ((), ())), preferred_element_type=F32)
            packed[t, :, :, j * cols : (j + 1) * cols] = rowset.astype(BF16).reshape(PAIRS, CAP, cols)

    copies[2].wait()
    copies[3].wait()
    norm_pack(0, xin)
    pl.semaphore_wait(barrier, count)

    def landing(t):
        return (xprev, wprev, ret) if t < TICKS - 1 else (x_out, w_out, r_out)

    def arrive(t):
        at, wt, rt = landing(t)
        remote(at, at, nx_send.at[t], nx_recv.at[t], nxt, p).wait_recv()
        remote(wt, wt, nw_send.at[t], nw_recv.at[t], nxt, p).wait_recv()
        remote(rt, rt, ret_send.at[t], ret_recv.at[t], nxt, p).wait_recv()

    def pair_of(c):
        return row_of(NEAR[CHUNKS[c][0]]) // 2

    def kind_of(c):
        return (0, 2 - b, 1 + b, 3)[c]

    for t in range(TICKS):
        if t > 0:
            arrive(t - 1)
            for j in range(GROUP):
                span = slice(j * cols, (j + 1) * cols)
                xcur[:, span] = combined(xprev[:, span], wprev[...], ret[:, :, span])
            norm_pack(t, xcur)

        def cell(k, column):
            row = row_of(NEAR[k])
            return rbuf.at[t, row // 2, lax.rem(row, 2) * XS + column]

        def send(k):
            mine = cell(k, x)
            if k > 0:
                remote(mine, mine, y_send.at[t], y_recv.at[t * 8 + k], s, home + right).wait_recv()
            remote(mine, mine, xf_send.at[t], xf_recv.at[t, k, 0], s, home + right).start()
            remote(mine, mine, xf_send.at[t], xf_recv.at[t, k, 1], s, home + left).start()
            if NEAR[k] < 0:
                onward = NEAR.index(1 - NEAR[k])
                remote(mine, mine, y_send.at[t], y_recv.at[t * 8 + onward], s, row_of(1) * XS + x).start()

        def relay(k):
            from_left, from_right = cell(k, left), cell(k, right)
            remote(from_left, from_left, xf_send.at[t], xf_recv.at[t, k, 0], s, home + right).wait_recv()
            part = from_left.at[:, 0:half]
            remote(part, part, xh_send.at[t], xh_recv.at[t, k, 0], s, home + right).start()
            remote(from_right, from_right, xf_send.at[t], xf_recv.at[t, k, 1], s, home + left).wait_recv()
            part = from_right.at[:, half:width]
            remote(part, part, xh_send.at[t], xh_recv.at[t, k, 1], s, home + left).start()

        def gate_up(c):
            if t == 0 and c == 0:
                copies[4].wait()
                copies[5].wait()
            for k in CHUNKS[c]:
                far = cell(k, across)
                for side, span in ((0, (0, half)), (1, (half, width))):
                    part = far.at[:, span[0] : span[1]]
                    remote(part, part, xh_send.at[t], xh_recv.at[t, k, side], s, home + right).wait_recv()
            pp = pair_of(c)
            taken = rbuf[t, pp].reshape(GROUP * CAP, width)
            both = jnp.dot(taken, wgu[...], preferred_element_type=F32)
            gate, up = both[:, 0:128], both[:, 128:256]
            act[t, q, pp] = (gate / (1.0 + jnp.exp(-gate)) * up).astype(BF16)
            mine = act.at[t, q, pp]
            for step in (1, 3, 5, 7, 4, 2, 6):
                other = lax.rem(q + step, GROUP)
                remote(
                    mine, mine, act_send.at[t], act_recv.at[t * PAIRS + kind_of(c)], s, pr * GROUP + other
                ).start()

        def resplit(other):
            remote(
                wd.at[0, :, pl.ds(pl.multiple_of(other * cols, 128), cols)], wd2.at[q],
                wd_send.at[0], wd_recv.at[0], s, pr * GROUP + other,
            ).start()

        def down(c):
            pp = lax.rem(pr + (0, 1, 3, 2)[c], PAIRS)
            kind = (0, 1, 2, 3)[c]
            block = act.at[t, 0:7, 0]
            remote(block, block, act_send.at[t], act_recv.at[t * PAIRS + kind], s, pr * GROUP).wait_recv()
            units = jnp.concatenate([act[t, k, pp] for k in range(GROUP)], axis=1)
            full = jnp.dot(units, wd2[...].reshape(GROUP * 128, cols), preferred_element_type=F32)
            outb[t, pp] = full.astype(BF16).reshape(GROUP, CAP, cols)
            for step in range(GROUP):
                owner = lax.rem(q + step, GROUP)
                remote(
                    outb.at[t, pp, owner], there_r.at[pr, :, pl.ds(pl.multiple_of(q * cols, 128), cols)],
                    ret_send.at[t], ret_recv.at[t], nxt, pp * GROUP + owner,
                ).start()

        for offset, seen in STEPS_OUT:
            target = row_of(offset)
            remote(
                packed.at[t, target // 2], rbuf.at[t, pr, q], y_send.at[t], y_recv.at[t * 8 + NEAR.index(seen)],
                s, target * XS + x,
            ).start()
        rbuf[t, pr, q] = packed[t, pr]
        there_x, there_w, there_r = landing(t)
        remote(hid.at[0] if t == 0 else xcur, there_x, nx_send.at[t], nx_recv.at[t], nxt, p).start()
        remote(wloc.at[t], there_w, nw_send.at[t], nw_recv.at[t], nxt, p).start()

        for step in PLAN[t]:
            what, arg = step[0], step[1:]
            if what == "S":
                send(int(arg))
            elif what == "R":
                relay(int(arg))
            elif what == "G":
                gate_up(int(arg))
            elif what == "D":
                down(int(arg))
            elif what == "V":
                copies[6].wait()
                remote(wd2.at[0:7], wd2.at[0:7], wd_send.at[0], wd_recv.at[0], s, pr * GROUP).wait_recv()
            else:
                column = {"+1": right, "-1": left, "2": across, "m": x, "+5": right, "-5": left, "6": across}[arg]
                resplit((b if arg in ("+1", "-1", "2") else 1 - b) * XS + column)

    arrive(TICKS - 1)
    for t in range(TICKS):
        remote(rbuf.at[t, 0, 0:7], rbuf.at[t, 0, 0:7], y_send.at[t], y_recv.at[0], s, p).wait_send()
        remote(rbuf.at[t, 0:2], rbuf.at[t, 0:2], xf_send.at[t], xf_recv.at[t, 0, 0], s, p).wait_send()
        remote(rbuf.at[t, 0], rbuf.at[t, 0], xh_send.at[t], xh_recv.at[t, 0, 0], s, p).wait_send()
        remote(act.at[t, 0:7], act.at[t, 0:7], act_send.at[t], act_recv.at[0], s, p).wait_send()
        remote(ret, ret, ret_send.at[t], ret_recv.at[t], s, p).wait_send()
        remote(xprev, xprev, nx_send.at[t], nx_recv.at[t], s, p).wait_send()
        remote(wprev, wprev, nw_send.at[t], nw_recv.at[t], s, p).wait_send()
    remote(wd2.at[0:7], wd2.at[0:7], wd_send.at[0], wd_recv.at[0], s, p).wait_send()


def body(hidden, expert_ids, route_weights, norm_gain, w_gate, w_up, w_down):
    _, rows, width = hidden.shape
    cols = width // GROUP
    top = expert_ids.shape[-1]
    dma = pltpu.SemaphoreType.DMA
    landed = pl.pallas_call(
        kernel,
        out_shape=(
            jax.ShapeDtypeStruct((rows, width), BF16),
            jax.ShapeDtypeStruct((rows, 128), BF16),
            jax.ShapeDtypeStruct((PAIRS, CAP, width), BF16),
        ),
        in_specs=[pl.BlockSpec(memory_space=pl.ANY)] * 7,
        out_specs=[pl.BlockSpec(memory_space=pl.ANY)] * 3,
        scratch_shapes=[
            pltpu.VMEM((rows, width), BF16),
            pltpu.VMEM((TICKS, top, rows), jnp.int32),
            pltpu.VMEM((TICKS, top, rows), F32),
            pltpu.VMEM((1, width), BF16),
            pltpu.VMEM((width, 256), BF16),
            pltpu.VMEM((GROUP, 128, cols), BF16),
            pltpu.VMEM((rows, width), BF16),
            pltpu.VMEM((rows, width), BF16),
            pltpu.VMEM((TICKS, rows, 128), BF16),
            pltpu.VMEM((rows, 128), BF16),
            pltpu.VMEM((TICKS, rows, 128), BF16),
            pltpu.VMEM((TICKS, PAIRS, CAP, width), BF16),
            pltpu.VMEM((TICKS, PAIRS, GROUP, CAP, width), BF16),
            pltpu.VMEM((TICKS, GROUP, PAIRS, GROUP * CAP, 128), BF16),
            pltpu.VMEM((TICKS, PAIRS, GROUP, CAP, cols), BF16),
            pltpu.VMEM((PAIRS, CAP, width), BF16),
            dma((7,)),
            dma((1,)), dma((1,)),
            dma((TICKS,)), dma((TICKS * 8,)),
            dma((TICKS,)), dma((TICKS, 8, 2)),
            dma((TICKS,)), dma((TICKS, 8, 2)),
            dma((TICKS,)), dma((TICKS * PAIRS,)),
            dma((TICKS,)), dma((TICKS,)),
            dma((TICKS,)), dma((TICKS,)),
            dma((TICKS,)), dma((TICKS,)),
        ],
        compiler_params=pltpu.CompilerParams(collective_id=0, has_side_effects=True),
    )(hidden, jnp.swapaxes(expert_ids, 2, 3), jnp.swapaxes(route_weights, 2, 3), norm_gain, w_gate, w_up, w_down)
    part = width // 2
    return pl.pallas_call(
        finish,
        grid=(2,),
        out_shape=jax.ShapeDtypeStruct(hidden.shape, BF16),
        in_specs=[
            pl.BlockSpec((rows, part), lambda i: (0, i)),
            pl.BlockSpec((rows, 128), lambda i: (0, 0)),
            pl.BlockSpec((PAIRS, CAP, part), lambda i: (0, 0, i)),
        ],
        out_specs=pl.BlockSpec((1, rows, part), lambda i: (0, 0, i)),
    )(*landed)


def solution(mesh):
    return jax.shard_map(
        body,
        mesh=mesh,
        in_specs=(
            P("segment", "expert", None),
            P(None, "segment", "expert", None),
            P(None, "segment", "expert", None),
            P("segment", None),
            P("segment", None, "expert"),
            P("segment", None, "expert"),
            P("segment", "expert", None),
        ),
        out_specs=P("segment", "expert", None),
        check_vma=False,
    )
```

```python
import functools

import jax
import jax.numpy as jnp
from jax import lax
from jax.experimental import pallas as pl
from jax.experimental.pallas import tpu as pltpu
from jax.sharding import PartitionSpec as P

EPS = 1e-06
TICKS = 2
PAIRS = 4
GROUP = 8
XS = 4
CAP = 8
MESH = pl.DeviceIdType.MESH
F32 = jnp.float32
BF16 = jnp.bfloat16

def combined(x, w, r):
    r = r.reshape(PAIRS * CAP, r.shape[-1])
    branch = jnp.dot(w[:, 0:64], jnp.concatenate([r, r], axis=0), preferred_element_type=F32)
    return (x.astype(F32) + branch).astype(BF16)


def finish(x_ref, w_ref, r_ref, o_ref):
    step = 512
    for j in range(x_ref.shape[1] // step):
        span = slice(j * step, (j + 1) * step)
        o_ref[0, :, span] = combined(x_ref[:, span], w_ref[...], r_ref[:, :, span])


NEAR = (0, -1, -2, -3, 2, 3, 1, 4)
WHOLE, HANDED = 3, 7
CHUNKS = ((0, 6), (1, 2), (4, 5), (3, 7))
STEPS_OUT = ((1, 1), (-1, -1), (2, -2), (-3, -3))
PLAN = (
    ("S0", "W+1", "W-1", "S1", "S2", "Wm", "R0", "S3", "R1", "S4", "W+5", "W-5", "R2", "S5", "R3", "S6", "G1", "R4", "W2", "F", "R5", "G3", "R6", "W6", "G2", "G0", "V", "D3", "D1", "D2", "D0"),
    ("S0", "S1", "S2", "R0", "S3", "R1", "S4", "R2", "S5", "R3", "S6", "G1", "R4", "F", "R5", "G3", "R6", "G2", "D3", "G0", "D1", "D2", "D0"),
)


def kernel(
    hid, ids, rw, gain, wg, wu, wd, x_out, w_out, r_out,
    xin, ids_v, rw_v, gain_v, wgu, wd2, xcur, xprev, wloc, wprev, place, packed, rbuf, act, outb, ret,
    loc_sem, wd_send, wd_recv, y_send, y_recv, xf_send, xf_recv, xh_send, xh_recv,
    act_send, act_recv, ret_send, ret_recv, nx_send, nx_recv, nw_send, nw_recv,
):
    segments = lax.axis_size("segment")
    rows, width = xcur.shape
    half = width // 2
    cols = width // GROUP
    s = lax.axis_index("segment")
    p = lax.axis_index("expert")
    pr = p // GROUP
    q = p % GROUP
    b = q // XS
    x = q % XS
    y = p // XS
    nxt = lax.rem(s + 1, segments)
    prv = lax.rem(s + segments - 1, segments)
    right = lax.rem(x + 1, XS)
    left = lax.rem(x + XS - 1, XS)
    across = lax.rem(x + 2, XS)
    home = y * XS
    sign = 1 - 2 * b

    def row_of(offset):
        return lax.rem(y + sign * offset + 16, 8)

    loads = [
        (ids.at[:, 0], ids_v),
        (rw.at[:, 0], rw_v),
        (hid.at[0], xin),
        (gain, gain_v),
        (wg.at[0], wgu.at[:, 0:128]),
        (wu.at[0], wgu.at[:, 128:256]),
        (wd.at[0, :, pl.ds(pl.multiple_of(q * cols, 128), cols)], wd2.at[q]),
    ]
    copies = [pltpu.make_async_copy(a, c, loc_sem.at[i]) for i, (a, c) in enumerate(loads)]
    for c in copies[:4]:
        c.start()

    barrier = pltpu.get_barrier_semaphore()

    def greet(seg, exp):
        pl.semaphore_signal(barrier, inc=1, device_id=(seg, exp), device_id_type=MESH)

    greet(prv, p)
    for step in range(1, GROUP):
        greet(s, pr * GROUP + lax.rem(q + step, GROUP))
    for offset in (-1, -2, -3):
        greet(s, row_of(offset) * XS + x)
    count = 1 + GROUP - 1 + 3
    for c in copies[4:]:
        c.start()

    def remote(src, dst, send, recv, seg, exp):
        return pltpu.make_async_remote_copy(
            src_ref=src, dst_ref=dst, send_sem=send, recv_sem=recv, device_id=(seg, exp), device_id_type=MESH
        )

    copies[0].wait()
    copies[1].wait()
    lane = lax.broadcasted_iota(jnp.int32, (rows, 128), 1)
    lane_e = lax.rem(lane, 32) // CAP
    lane_c = lax.rem(lane, CAP)
    tri = (
        lax.broadcasted_iota(jnp.int32, (rows, rows), 0) >= lax.broadcasted_iota(jnp.int32, (rows, rows), 1)
    ).astype(F32).astype(BF16)
    for t in range(TICKS):
        share = jnp.zeros((rows, 128), F32)
        member = jnp.zeros((rows, 128), F32)
        idt = jnp.transpose(ids_v[t])
        rwt = jnp.transpose(rw_v[t])
        for k in range(idt.shape[1]):
            hit = idt[:, k : k + 1] == lane_e
            share = share + jnp.where(hit, rwt[:, k : k + 1], F32(0.0))
            member = jnp.where(hit, F32(1.0), member)
        rank = jnp.dot(tri, member.astype(BF16), preferred_element_type=F32)
        placed = jnp.where(rank == (lane_c + 1).astype(F32), member, F32(0.0))
        place[t] = placed.astype(BF16)
        weight = placed * share
        high = weight.astype(BF16)
        low = (weight - high.astype(F32)).astype(BF16)
        zero = jnp.zeros_like(weight)
        wloc[t] = jnp.where(lane < 32, high.astype(F32), jnp.where(lane < 64, low.astype(F32), zero)).astype(BF16)

    def norm_pack(t, source):
        total = jnp.zeros((rows, 1), F32)
        for j in range(GROUP):
            v = source[:, j * cols : (j + 1) * cols].astype(F32)
            total = total + jnp.sum(v * v, axis=-1, keepdims=True)
        scale = lax.rsqrt(total / width + EPS)
        pick = place[t][:, 0:32]
        for j in range(GROUP):
            v = source[:, j * cols : (j + 1) * cols].astype(F32)
            g = gain_v[0:1, j * cols : (j + 1) * cols].astype(F32)
            normed = (v * scale * g).astype(BF16)
            rowset = lax.dot_general(pick, normed, (((0,), (0,)), ((), ())), preferred_element_type=F32)
            packed[t, :, :, j * cols : (j + 1) * cols] = rowset.astype(BF16).reshape(PAIRS, CAP, cols)

    copies[2].wait()
    copies[3].wait()
    norm_pack(0, xin)
    pl.semaphore_wait(barrier, count)

    def landing(t):
        return (xprev, wprev, ret) if t < TICKS - 1 else (x_out, w_out, r_out)

    def arrive(t):
        at, wt, rt = landing(t)
        remote(at, at, nx_send.at[t], nx_recv.at[t], nxt, p).wait_recv()
        remote(wt, wt, nw_send.at[t], nw_recv.at[t], nxt, p).wait_recv()
        remote(rt, rt, ret_send.at[t], ret_recv.at[t], nxt, p).wait_recv()

    def pair_of(c):
        return row_of(NEAR[CHUNKS[c][0]]) // 2

    def kind_of(c):
        return (0, 2 - b, 1 + b, 3)[c]

    for t in range(TICKS):
        if t > 0:
            arrive(t - 1)
            for j in range(GROUP):
                span = slice(j * cols, (j + 1) * cols)
                xcur[:, span] = combined(xprev[:, span], wprev[...], ret[:, :, span])
            norm_pack(t, xcur)

        def cell(k, column):
            row = row_of(NEAR[k])
            return rbuf.at[t, row // 2, lax.rem(row, 2) * XS + column]

        def hand(block, arrived):
            remote(block, block, y_send.at[t], arrived, s, row_of(1) * XS + x).start()

        def far_halves(k):
            far = cell(k, across)
            for side, span in ((0, (0, half)), (1, (half, width))):
                part = far.at[:, span[0] : span[1]]
                remote(part, part, xh_send.at[t], xh_recv.at[t, k, side], s, home + right).wait_recv()

        def hand_far():
            far_halves(WHOLE)
            hand(cell(WHOLE, across), xh_recv.at[t, HANDED, 0])

        def send(k):
            mine = cell(k, x)
            if k > 0:
                remote(mine, mine, y_send.at[t], y_recv.at[t * 8 + k], s, home + right).wait_recv()
            remote(mine, mine, xf_send.at[t], xf_recv.at[t, k, 0], s, home + right).start()
            remote(mine, mine, xf_send.at[t], xf_recv.at[t, k, 1], s, home + left).start()
            if NEAR[k] < 0:
                onward = NEAR.index(1 - NEAR[k])
                hand(mine, y_recv.at[t * 8 + onward])

        def relay(k):
            from_left, from_right = cell(k, left), cell(k, right)
            remote(from_left, from_left, xf_send.at[t], xf_recv.at[t, k, 0], s, home + right).wait_recv()
            part = from_left.at[:, 0:half]
            remote(part, part, xh_send.at[t], xh_recv.at[t, k, 0], s, home + right).start()
            remote(from_right, from_right, xf_send.at[t], xf_recv.at[t, k, 1], s, home + left).wait_recv()
            part = from_right.at[:, half:width]
            remote(part, part, xh_send.at[t], xh_recv.at[t, k, 1], s, home + left).start()
            if k == WHOLE:
                hand(from_left, xf_recv.at[t, HANDED, 0])
                hand(from_right, xf_recv.at[t, HANDED, 1])

        def gate_up(c):
            if t == 0 and c == 1:
                copies[4].wait()
                copies[5].wait()
            for k in CHUNKS[c]:
                if k == HANDED:
                    for column, arrived in (
                        (x, y_recv.at[t * 8 + k]),
                        (left, xf_recv.at[t, k, 0]),
                        (right, xf_recv.at[t, k, 1]),
                        (across, xh_recv.at[t, k, 0]),
                    ):
                        block = cell(k, column)
                        remote(block, block, y_send.at[t], arrived, s, row_of(1) * XS + x).wait_recv()
                elif k != WHOLE:
                    far_halves(k)
            pp = pair_of(c)
            taken = rbuf[t, pp].reshape(GROUP * CAP, width)
            both = jnp.dot(taken, wgu[...], preferred_element_type=F32)
            gate, up = both[:, 0:128], both[:, 128:256]
            act[t, q, pp] = (gate / (1.0 + jnp.exp(-gate)) * up).astype(BF16)
            mine = act.at[t, q, pp]
            for step in (1, 3, 5, 7, 4, 2, 6):
                other = lax.rem(q + step, GROUP)
                remote(
                    mine, mine, act_send.at[t], act_recv.at[t * PAIRS + kind_of(c)], s, pr * GROUP + other
                ).start()

        def resplit(other):
            remote(
                wd.at[0, :, pl.ds(pl.multiple_of(other * cols, 128), cols)], wd2.at[q],
                wd_send.at[0], wd_recv.at[0], s, pr * GROUP + other,
            ).start()

        def down(c):
            pp = lax.rem(pr + (0, 1, 3, 2)[c], PAIRS)
            kind = (0, 1, 2, 3)[c]
            block = act.at[t, 0:7, 0]
            remote(block, block, act_send.at[t], act_recv.at[t * PAIRS + kind], s, pr * GROUP).wait_recv()
            units = jnp.concatenate([act[t, k, pp] for k in range(GROUP)], axis=1)
            full = jnp.dot(units, wd2[...].reshape(GROUP * 128, cols), preferred_element_type=F32)
            outb[t, pp] = full.astype(BF16).reshape(GROUP, CAP, cols)
            for step in range(GROUP):
                owner = lax.rem(q + step, GROUP)
                remote(
                    outb.at[t, pp, owner], there_r.at[pr, :, pl.ds(pl.multiple_of(q * cols, 128), cols)],
                    ret_send.at[t], ret_recv.at[t], nxt, pp * GROUP + owner,
                ).start()

        for offset, seen in STEPS_OUT:
            target = row_of(offset)
            remote(
                packed.at[t, target // 2], rbuf.at[t, pr, q], y_send.at[t], y_recv.at[t * 8 + NEAR.index(seen)],
                s, target * XS + x,
            ).start()
        rbuf[t, pr, q] = packed[t, pr]
        there_x, there_w, there_r = landing(t)
        remote(hid.at[0] if t == 0 else xcur, there_x, nx_send.at[t], nx_recv.at[t], nxt, p).start()
        remote(wloc.at[t], there_w, nw_send.at[t], nw_recv.at[t], nxt, p).start()

        for step in PLAN[t]:
            what, arg = step[0], step[1:]
            if what == "S":
                send(int(arg))
            elif what == "R":
                relay(int(arg))
            elif what == "F":
                hand_far()
            elif what == "G":
                gate_up(int(arg))
            elif what == "D":
                down(int(arg))
            elif what == "V":
                copies[6].wait()
                remote(wd2.at[0:7], wd2.at[0:7], wd_send.at[0], wd_recv.at[0], s, pr * GROUP).wait_recv()
            else:
                column = {"+1": right, "-1": left, "2": across, "m": x, "+5": right, "-5": left, "6": across}[arg]
                resplit((b if arg in ("+1", "-1", "2") else 1 - b) * XS + column)

    arrive(TICKS - 1)
    for t in range(TICKS):
        remote(rbuf.at[t, 0:2, 0:5], rbuf.at[t, 0:2, 0:5], y_send.at[t], y_recv.at[0], s, p).wait_send()
        remote(rbuf.at[t, 0:2, 0:7], rbuf.at[t, 0:2, 0:7], xf_send.at[t], xf_recv.at[t, 0, 0], s, p).wait_send()
        remote(rbuf.at[t, 0, 0:7], rbuf.at[t, 0, 0:7], xh_send.at[t], xh_recv.at[t, 0, 0], s, p).wait_send()
        remote(act.at[t, 0:7], act.at[t, 0:7], act_send.at[t], act_recv.at[0], s, p).wait_send()
        remote(ret, ret, ret_send.at[t], ret_recv.at[t], s, p).wait_send()
        remote(xprev, xprev, nx_send.at[t], nx_recv.at[t], s, p).wait_send()
        remote(wprev, wprev, nw_send.at[t], nw_recv.at[t], s, p).wait_send()
    remote(wd2.at[0:7], wd2.at[0:7], wd_send.at[0], wd_recv.at[0], s, p).wait_send()


def body(hidden, expert_ids, route_weights, norm_gain, w_gate, w_up, w_down):
    _, rows, width = hidden.shape
    cols = width // GROUP
    top = expert_ids.shape[-1]
    dma = pltpu.SemaphoreType.DMA
    landed = pl.pallas_call(
        kernel,
        out_shape=(
            jax.ShapeDtypeStruct((rows, width), BF16),
            jax.ShapeDtypeStruct((rows, 128), BF16),
            jax.ShapeDtypeStruct((PAIRS, CAP, width), BF16),
        ),
        in_specs=[pl.BlockSpec(memory_space=pl.ANY)] * 7,
        out_specs=[pl.BlockSpec(memory_space=pl.ANY)] * 3,
        scratch_shapes=[
            pltpu.VMEM((rows, width), BF16),
            pltpu.VMEM((TICKS, top, rows), jnp.int32),
            pltpu.VMEM((TICKS, top, rows), F32),
            pltpu.VMEM((1, width), BF16),
            pltpu.VMEM((width, 256), BF16),
            pltpu.VMEM((GROUP, 128, cols), BF16),
            pltpu.VMEM((rows, width), BF16),
            pltpu.VMEM((rows, width), BF16),
            pltpu.VMEM((TICKS, rows, 128), BF16),
            pltpu.VMEM((rows, 128), BF16),
            pltpu.VMEM((TICKS, rows, 128), BF16),
            pltpu.VMEM((TICKS, PAIRS, CAP, width), BF16),
            pltpu.VMEM((TICKS, PAIRS, GROUP, CAP, width), BF16),
            pltpu.VMEM((TICKS, GROUP, PAIRS, GROUP * CAP, 128), BF16),
            pltpu.VMEM((TICKS, PAIRS, GROUP, CAP, cols), BF16),
            pltpu.VMEM((PAIRS, CAP, width), BF16),
            dma((7,)),
            dma((1,)), dma((1,)),
            dma((TICKS,)), dma((TICKS * 8,)),
            dma((TICKS,)), dma((TICKS, 8, 2)),
            dma((TICKS,)), dma((TICKS, 8, 2)),
            dma((TICKS,)), dma((TICKS * PAIRS,)),
            dma((TICKS,)), dma((TICKS,)),
            dma((TICKS,)), dma((TICKS,)),
            dma((TICKS,)), dma((TICKS,)),
        ],
        compiler_params=pltpu.CompilerParams(collective_id=0, has_side_effects=True),
    )(hidden, jnp.swapaxes(expert_ids, 2, 3), jnp.swapaxes(route_weights, 2, 3), norm_gain, w_gate, w_up, w_down)
    part = width // 2
    return pl.pallas_call(
        finish,
        grid=(2,),
        out_shape=jax.ShapeDtypeStruct(hidden.shape, BF16),
        in_specs=[
            pl.BlockSpec((rows, part), lambda i: (0, i)),
            pl.BlockSpec((rows, 128), lambda i: (0, 0)),
            pl.BlockSpec((PAIRS, CAP, part), lambda i: (0, 0, i)),
        ],
        out_specs=pl.BlockSpec((1, rows, part), lambda i: (0, 0, i)),
    )(*landed)


def solution(mesh):
    return jax.shard_map(
        body,
        mesh=mesh,
        in_specs=(
            P("segment", "expert", None),
            P(None, "segment", "expert", None),
            P(None, "segment", "expert", None),
            P("segment", None),
            P("segment", None, "expert"),
            P("segment", None, "expert"),
            P("segment", "expert", None),
        ),
        out_specs=P("segment", "expert", None),
        check_vma=False,
    )
```

```python
import functools

import jax
import jax.numpy as jnp
from jax import lax
from jax.experimental import pallas as pl
from jax.experimental.pallas import tpu as pltpu
from jax.sharding import PartitionSpec as P

EPS = 1e-06
TICKS = 2
PAIRS = 4
GROUP = 8
XS = 4
CAP = 8
MESH = pl.DeviceIdType.MESH
F32 = jnp.float32
BF16 = jnp.bfloat16

def combined(x, w, r):
    r = r.reshape(PAIRS * CAP, r.shape[-1])
    branch = jnp.dot(w[:, 0:64], jnp.concatenate([r, r], axis=0), preferred_element_type=F32)
    return (x.astype(F32) + branch).astype(BF16)


def finish(x_ref, w_ref, r_ref, o_ref):
    step = 512
    for j in range(x_ref.shape[1] // step):
        span = slice(j * step, (j + 1) * step)
        o_ref[0, :, span] = combined(x_ref[:, span], w_ref[...], r_ref[:, :, span])


NEAR = (0, -1, -2, -3, 2, 3, 1, 4)
WHOLE, HANDED = 3, 7
DIRECT = 6
CHUNKS = ((0, 6), (1, 2), (4, 5), (3, 7))
STEPS_OUT = ((1, 1), (-1, -1), (2, -2), (-3, -3))
PLAN = (
    ("S0", "W+1", "W-1", "S1", "S2", "Wm", "R0", "S3", "R1", "S4", "W+5", "W-5", "R2", "S5", "R3", "R4", "S6", "G1", "R5", "W2", "F", "W6", "G3", "G2", "G0", "V", "D3", "D1", "D2", "D0"),
    ("S0", "S1", "S2", "R0", "S3", "R1", "S4", "R2", "S5", "R3", "R4", "S6", "G1", "R5", "F", "G3", "G2", "G0", "D3", "D1", "D2", "D0"),
)


def kernel(
    hid, ids, rw, gain, wg, wu, wd, x_out, w_out, r_out,
    xin, ids_v, rw_v, gain_v, wgu, wd2, xcur, xprev, wloc, wprev, place, packed, rbuf, act, outb, ret,
    loc_sem, wd_send, wd_recv, y_send, y_recv, xf_send, xf_recv, xh_send, xh_recv,
    act_send, act_recv, ret_send, ret_recv, nx_send, nx_recv, nw_send, nw_recv,
):
    segments = lax.axis_size("segment")
    rows, width = xcur.shape
    half = width // 2
    cols = width // GROUP
    s = lax.axis_index("segment")
    p = lax.axis_index("expert")
    pr = p // GROUP
    q = p % GROUP
    b = q // XS
    x = q % XS
    y = p // XS
    nxt = lax.rem(s + 1, segments)
    prv = lax.rem(s + segments - 1, segments)
    right = lax.rem(x + 1, XS)
    left = lax.rem(x + XS - 1, XS)
    across = lax.rem(x + 2, XS)
    home = y * XS
    sign = 1 - 2 * b

    def row_of(offset):
        return lax.rem(y + sign * offset + 16, 8)

    loads = [
        (ids.at[:, 0], ids_v),
        (rw.at[:, 0], rw_v),
        (hid.at[0], xin),
        (gain, gain_v),
        (wg.at[0], wgu.at[:, 0:128]),
        (wu.at[0], wgu.at[:, 128:256]),
        (wd.at[0, :, pl.ds(pl.multiple_of(q * cols, 128), cols)], wd2.at[q]),
    ]
    copies = [pltpu.make_async_copy(a, c, loc_sem.at[i]) for i, (a, c) in enumerate(loads)]
    for c in copies[:4]:
        c.start()

    barrier = pltpu.get_barrier_semaphore()

    def greet(seg, exp):
        pl.semaphore_signal(barrier, inc=1, device_id=(seg, exp), device_id_type=MESH)

    greet(prv, p)
    for step in range(1, GROUP):
        greet(s, pr * GROUP + lax.rem(q + step, GROUP))
    for offset in (-1, -2, -3):
        greet(s, row_of(offset) * XS + x)
    count = 1 + GROUP - 1 + 3
    for c in copies[4:]:
        c.start()

    def remote(src, dst, send, recv, seg, exp):
        return pltpu.make_async_remote_copy(
            src_ref=src, dst_ref=dst, send_sem=send, recv_sem=recv, device_id=(seg, exp), device_id_type=MESH
        )

    copies[0].wait()
    copies[1].wait()
    lane = lax.broadcasted_iota(jnp.int32, (rows, 128), 1)
    lane_e = lax.rem(lane, 32) // CAP
    lane_c = lax.rem(lane, CAP)
    tri = (
        lax.broadcasted_iota(jnp.int32, (rows, rows), 0) >= lax.broadcasted_iota(jnp.int32, (rows, rows), 1)
    ).astype(F32).astype(BF16)
    for t in range(TICKS):
        share = jnp.zeros((rows, 128), F32)
        member = jnp.zeros((rows, 128), F32)
        idt = jnp.transpose(ids_v[t])
        rwt = jnp.transpose(rw_v[t])
        for k in range(idt.shape[1]):
            hit = idt[:, k : k + 1] == lane_e
            share = share + jnp.where(hit, rwt[:, k : k + 1], F32(0.0))
            member = jnp.where(hit, F32(1.0), member)
        rank = jnp.dot(tri, member.astype(BF16), preferred_element_type=F32)
        placed = jnp.where(rank == (lane_c + 1).astype(F32), member, F32(0.0))
        place[t] = placed.astype(BF16)
        weight = placed * share
        high = weight.astype(BF16)
        low = (weight - high.astype(F32)).astype(BF16)
        zero = jnp.zeros_like(weight)
        wloc[t] = jnp.where(lane < 32, high.astype(F32), jnp.where(lane < 64, low.astype(F32), zero)).astype(BF16)

    def norm_pack(t, source):
        total = jnp.zeros((rows, 1), F32)
        for j in range(GROUP):
            v = source[:, j * cols : (j + 1) * cols].astype(F32)
            total = total + jnp.sum(v * v, axis=-1, keepdims=True)
        scale = lax.rsqrt(total / width + EPS)
        pick = place[t][:, 0:32]
        for j in range(GROUP):
            v = source[:, j * cols : (j + 1) * cols].astype(F32)
            g = gain_v[0:1, j * cols : (j + 1) * cols].astype(F32)
            normed = (v * scale * g).astype(BF16)
            rowset = lax.dot_general(pick, normed, (((0,), (0,)), ((), ())), preferred_element_type=F32)
            packed[t, :, :, j * cols : (j + 1) * cols] = rowset.astype(BF16).reshape(PAIRS, CAP, cols)

    copies[2].wait()
    copies[3].wait()
    norm_pack(0, xin)
    pl.semaphore_wait(barrier, count)

    def landing(t):
        return (xprev, wprev, ret) if t < TICKS - 1 else (x_out, w_out, r_out)

    def arrive(t):
        at, wt, rt = landing(t)
        remote(at, at, nx_send.at[t], nx_recv.at[t], nxt, p).wait_recv()
        remote(wt, wt, nw_send.at[t], nw_recv.at[t], nxt, p).wait_recv()
        remote(rt, rt, ret_send.at[t], ret_recv.at[t], nxt, p).wait_recv()

    def pair_of(c):
        return row_of(NEAR[CHUNKS[c][0]]) // 2

    def kind_of(c):
        return (0, 2 - b, 1 + b, 3)[c]

    for t in range(TICKS):
        if t > 0:
            arrive(t - 1)
            for j in range(GROUP):
                span = slice(j * cols, (j + 1) * cols)
                xcur[:, span] = combined(xprev[:, span], wprev[...], ret[:, :, span])
            norm_pack(t, xcur)

        def cell(k, column):
            row = row_of(NEAR[k])
            return rbuf.at[t, row // 2, lax.rem(row, 2) * XS + column]

        def hand(block, arrived):
            remote(block, block, y_send.at[t], arrived, s, row_of(1) * XS + x).start()

        def far_halves(k):
            far = cell(k, across)
            if k == DIRECT:
                near_left, near_right = cell(k, left), cell(k, right)
                remote(near_left, near_left, xf_send.at[t], xf_recv.at[t, k, 0], s, home + right).wait_recv()
                remote(near_right, near_right, xf_send.at[t], xf_recv.at[t, k, 1], s, home + left).wait_recv()
                remote(far, far, xf_send.at[t], xh_recv.at[t, k, 0], s, home + right).wait_recv()
                return
            for side, span in ((0, (0, half)), (1, (half, width))):
                part = far.at[:, span[0] : span[1]]
                remote(part, part, xh_send.at[t], xh_recv.at[t, k, side], s, home + right).wait_recv()

        def hand_far():
            far_halves(WHOLE)
            hand(cell(WHOLE, across), xh_recv.at[t, HANDED, 0])

        def send(k):
            mine = cell(k, x)
            if k > 0:
                remote(mine, mine, y_send.at[t], y_recv.at[t * 8 + k], s, home + right).wait_recv()
            remote(mine, mine, xf_send.at[t], xf_recv.at[t, k, 0], s, home + right).start()
            remote(mine, mine, xf_send.at[t], xf_recv.at[t, k, 1], s, home + left).start()
            if k == DIRECT:
                remote(mine, mine, xf_send.at[t], xh_recv.at[t, k, 0], s, home + across).start()
            if NEAR[k] < 0:
                onward = NEAR.index(1 - NEAR[k])
                hand(mine, y_recv.at[t * 8 + onward])

        def relay(k):
            from_left, from_right = cell(k, left), cell(k, right)
            remote(from_left, from_left, xf_send.at[t], xf_recv.at[t, k, 0], s, home + right).wait_recv()
            part = from_left.at[:, 0:half]
            remote(part, part, xh_send.at[t], xh_recv.at[t, k, 0], s, home + right).start()
            remote(from_right, from_right, xf_send.at[t], xf_recv.at[t, k, 1], s, home + left).wait_recv()
            part = from_right.at[:, half:width]
            remote(part, part, xh_send.at[t], xh_recv.at[t, k, 1], s, home + left).start()
            if k == WHOLE:
                hand(from_left, xf_recv.at[t, HANDED, 0])
                hand(from_right, xf_recv.at[t, HANDED, 1])

        def gate_up(c):
            if t == 0 and c == 1:
                copies[4].wait()
                copies[5].wait()
            for k in CHUNKS[c]:
                if k == HANDED:
                    for column, arrived in (
                        (x, y_recv.at[t * 8 + k]),
                        (left, xf_recv.at[t, k, 0]),
                        (right, xf_recv.at[t, k, 1]),
                        (across, xh_recv.at[t, k, 0]),
                    ):
                        block = cell(k, column)
                        remote(block, block, y_send.at[t], arrived, s, row_of(1) * XS + x).wait_recv()
                elif k != WHOLE:
                    far_halves(k)
            pp = pair_of(c)
            taken = rbuf[t, pp].reshape(GROUP * CAP, width)
            both = jnp.dot(taken, wgu[...], preferred_element_type=F32)
            gate, up = both[:, 0:128], both[:, 128:256]
            act[t, q, pp] = (gate / (1.0 + jnp.exp(-gate)) * up).astype(BF16)
            mine = act.at[t, q, pp]
            for step in (1, 3, 5, 7, 4, 2, 6):
                other = lax.rem(q + step, GROUP)
                remote(
                    mine, mine, act_send.at[t], act_recv.at[t * PAIRS + kind_of(c)], s, pr * GROUP + other
                ).start()

        def resplit(other):
            remote(
                wd.at[0, :, pl.ds(pl.multiple_of(other * cols, 128), cols)], wd2.at[q],
                wd_send.at[0], wd_recv.at[0], s, pr * GROUP + other,
            ).start()

        def down(c):
            pp = lax.rem(pr + (0, 1, 3, 2)[c], PAIRS)
            kind = (0, 1, 2, 3)[c]
            block = act.at[t, 0:7, 0]
            remote(block, block, act_send.at[t], act_recv.at[t * PAIRS + kind], s, pr * GROUP).wait_recv()
            units = jnp.concatenate([act[t, k, pp] for k in range(GROUP)], axis=1)
            full = jnp.dot(units, wd2[...].reshape(GROUP * 128, cols), preferred_element_type=F32)
            outb[t, pp] = full.astype(BF16).reshape(GROUP, CAP, cols)
            for step in range(GROUP):
                owner = lax.rem(q + step, GROUP)
                remote(
                    outb.at[t, pp, owner], there_r.at[pr, :, pl.ds(pl.multiple_of(q * cols, 128), cols)],
                    ret_send.at[t], ret_recv.at[t], nxt, pp * GROUP + owner,
                ).start()

        for offset, seen in STEPS_OUT:
            target = row_of(offset)
            remote(
                packed.at[t, target // 2], rbuf.at[t, pr, q], y_send.at[t], y_recv.at[t * 8 + NEAR.index(seen)],
                s, target * XS + x,
            ).start()
        rbuf[t, pr, q] = packed[t, pr]
        there_x, there_w, there_r = landing(t)
        remote(hid.at[0] if t == 0 else xcur, there_x, nx_send.at[t], nx_recv.at[t], nxt, p).start()
        remote(wloc.at[t], there_w, nw_send.at[t], nw_recv.at[t], nxt, p).start()

        for step in PLAN[t]:
            what, arg = step[0], step[1:]
            if what == "S":
                send(int(arg))
            elif what == "R":
                relay(int(arg))
            elif what == "F":
                hand_far()
            elif what == "G":
                gate_up(int(arg))
            elif what == "D":
                down(int(arg))
            elif what == "V":
                copies[6].wait()
                remote(wd2.at[0:7], wd2.at[0:7], wd_send.at[0], wd_recv.at[0], s, pr * GROUP).wait_recv()
            else:
                column = {"+1": right, "-1": left, "2": across, "m": x, "+5": right, "-5": left, "6": across}[arg]
                resplit((b if arg in ("+1", "-1", "2") else 1 - b) * XS + column)

    arrive(TICKS - 1)
    for t in range(TICKS):
        remote(rbuf.at[t, 0:2, 0:5], rbuf.at[t, 0:2, 0:5], y_send.at[t], y_recv.at[0], s, p).wait_send()
        remote(rbuf.at[t, 0:3, 0:5], rbuf.at[t, 0:3, 0:5], xf_send.at[t], xf_recv.at[t, 0, 0], s, p).wait_send()
        remote(rbuf.at[t, 0, 0:6], rbuf.at[t, 0, 0:6], xh_send.at[t], xh_recv.at[t, 0, 0], s, p).wait_send()
        remote(act.at[t, 0:7], act.at[t, 0:7], act_send.at[t], act_recv.at[0], s, p).wait_send()
        remote(ret, ret, ret_send.at[t], ret_recv.at[t], s, p).wait_send()
        remote(xprev, xprev, nx_send.at[t], nx_recv.at[t], s, p).wait_send()
        remote(wprev, wprev, nw_send.at[t], nw_recv.at[t], s, p).wait_send()
    remote(wd2.at[0:7], wd2.at[0:7], wd_send.at[0], wd_recv.at[0], s, p).wait_send()


def body(hidden, expert_ids, route_weights, norm_gain, w_gate, w_up, w_down):
    _, rows, width = hidden.shape
    cols = width // GROUP
    top = expert_ids.shape[-1]
    dma = pltpu.SemaphoreType.DMA
    landed = pl.pallas_call(
        kernel,
        out_shape=(
            jax.ShapeDtypeStruct((rows, width), BF16),
            jax.ShapeDtypeStruct((rows, 128), BF16),
            jax.ShapeDtypeStruct((PAIRS, CAP, width), BF16),
        ),
        in_specs=[pl.BlockSpec(memory_space=pl.ANY)] * 7,
        out_specs=[pl.BlockSpec(memory_space=pl.ANY)] * 3,
        scratch_shapes=[
            pltpu.VMEM((rows, width), BF16),
            pltpu.VMEM((TICKS, top, rows), jnp.int32),
            pltpu.VMEM((TICKS, top, rows), F32),
            pltpu.VMEM((1, width), BF16),
            pltpu.VMEM((width, 256), BF16),
            pltpu.VMEM((GROUP, 128, cols), BF16),
            pltpu.VMEM((rows, width), BF16),
            pltpu.VMEM((rows, width), BF16),
            pltpu.VMEM((TICKS, rows, 128), BF16),
            pltpu.VMEM((rows, 128), BF16),
            pltpu.VMEM((TICKS, rows, 128), BF16),
            pltpu.VMEM((TICKS, PAIRS, CAP, width), BF16),
            pltpu.VMEM((TICKS, PAIRS, GROUP, CAP, width), BF16),
            pltpu.VMEM((TICKS, GROUP, PAIRS, GROUP * CAP, 128), BF16),
            pltpu.VMEM((TICKS, PAIRS, GROUP, CAP, cols), BF16),
            pltpu.VMEM((PAIRS, CAP, width), BF16),
            dma((7,)),
            dma((1,)), dma((1,)),
            dma((TICKS,)), dma((TICKS * 8,)),
            dma((TICKS,)), dma((TICKS, 8, 2)),
            dma((TICKS,)), dma((TICKS, 8, 2)),
            dma((TICKS,)), dma((TICKS * PAIRS,)),
            dma((TICKS,)), dma((TICKS,)),
            dma((TICKS,)), dma((TICKS,)),
            dma((TICKS,)), dma((TICKS,)),
        ],
        compiler_params=pltpu.CompilerParams(collective_id=0, has_side_effects=True),
    )(hidden, jnp.swapaxes(expert_ids, 2, 3), jnp.swapaxes(route_weights, 2, 3), norm_gain, w_gate, w_up, w_down)
    part = width // 2
    return pl.pallas_call(
        finish,
        grid=(2,),
        out_shape=jax.ShapeDtypeStruct(hidden.shape, BF16),
        in_specs=[
            pl.BlockSpec((rows, part), lambda i: (0, i)),
            pl.BlockSpec((rows, 128), lambda i: (0, 0)),
            pl.BlockSpec((PAIRS, CAP, part), lambda i: (0, 0, i)),
        ],
        out_specs=pl.BlockSpec((1, rows, part), lambda i: (0, 0, i)),
    )(*landed)


def solution(mesh):
    return jax.shard_map(
        body,
        mesh=mesh,
        in_specs=(
            P("segment", "expert", None),
            P(None, "segment", "expert", None),
            P(None, "segment", "expert", None),
            P("segment", None),
            P("segment", None, "expert"),
            P("segment", None, "expert"),
            P("segment", "expert", None),
        ),
        out_specs=P("segment", "expert", None),
        check_vma=False,
    )
```

```python
import functools

import jax
import jax.numpy as jnp
from jax import lax
from jax.experimental import pallas as pl
from jax.experimental.pallas import tpu as pltpu
from jax.sharding import PartitionSpec as P

EPS = 1e-06
TICKS = 2
PAIRS = 4
GROUP = 8
XS = 4
CAP = 8
MESH = pl.DeviceIdType.MESH
F32 = jnp.float32
BF16 = jnp.bfloat16

def combined(x, w, r):
    r = r.reshape(PAIRS * CAP, r.shape[-1])
    branch = jnp.dot(w[:, 0:64], jnp.concatenate([r, r], axis=0), preferred_element_type=F32)
    return (x.astype(F32) + branch).astype(BF16)


def finish(x_ref, w_ref, r_ref, o_ref):
    step = 512
    for j in range(x_ref.shape[1] // step):
        span = slice(j * step, (j + 1) * step)
        o_ref[0, :, span] = combined(x_ref[:, span], w_ref[...], r_ref[:, :, span])


NEAR = (0, -1, -2, -3, 2, 3, 1, 4)
WHOLE, HANDED = 3, 7
CHUNKS = ((0, 6), (1, 2), (4, 5), (3, 7))
STEPS_OUT = ((1, 1), (-1, -1), (2, -2), (-3, -3))
PLAN = (
    ("S0", "W+1", "W-1", "S1", "S2", "Wm", "R0", "S3", "R1", "S4", "W+5", "W-5", "R2", "S5", "R3", "S6", "G1", "R4", "W2", "F", "R5", "G3", "R6", "W6", "G2", "G0", "V", "D3", "D1", "D2", "D0"),
    ("S0", "S1", "S2", "R0", "S3", "R1", "S4", "R2", "S5", "R3", "S6", "G1", "R4", "F", "R5", "G3", "R6", "G2", "G0", "D3", "D1", "D2", "D0"),
)


def kernel(
    hid, ids, rw, gain, wg, wu, wd, x_out, w_out, r_out,
    xin, ids_v, rw_v, gain_v, wgu, wd2, xcur, xprev, wloc, wprev, place, packed, rbuf, act, outb, ret,
    loc_sem, wd_send, wd_recv, y_send, y_recv, xf_send, xf_recv, xh_send, xh_recv,
    act_send, act_recv, ret_send, ret_recv, nx_send, nx_recv, nw_send, nw_recv,
):
    segments = lax.axis_size("segment")
    rows, width = xcur.shape
    half = width // 2
    cols = width // GROUP
    s = lax.axis_index("segment")
    p = lax.axis_index("expert")
    pr = p // GROUP
    q = p % GROUP
    b = q // XS
    x = q % XS
    y = p // XS
    nxt = lax.rem(s + 1, segments)
    prv = lax.rem(s + segments - 1, segments)
    right = lax.rem(x + 1, XS)
    left = lax.rem(x + XS - 1, XS)
    across = lax.rem(x + 2, XS)
    home = y * XS
    sign = 1 - 2 * b

    def row_of(offset):
        return lax.rem(y + sign * offset + 16, 8)

    loads = [
        (ids.at[:, 0], ids_v),
        (rw.at[:, 0], rw_v),
        (hid.at[0], xin),
        (gain, gain_v),
        (wg.at[0], wgu.at[:, 0:128]),
        (wu.at[0], wgu.at[:, 128:256]),
        (wd.at[0, :, pl.ds(pl.multiple_of(q * cols, 128), cols)], wd2.at[q]),
    ]
    copies = [pltpu.make_async_copy(a, c, loc_sem.at[i]) for i, (a, c) in enumerate(loads)]
    for c in copies[:4]:
        c.start()

    barrier = pltpu.get_barrier_semaphore()

    def greet(seg, exp):
        pl.semaphore_signal(barrier, inc=1, device_id=(seg, exp), device_id_type=MESH)

    greet(prv, p)
    for step in range(1, GROUP):
        greet(s, pr * GROUP + lax.rem(q + step, GROUP))
    for offset in (-1, -2, -3):
        greet(s, row_of(offset) * XS + x)
    count = 1 + GROUP - 1 + 3
    for c in copies[4:]:
        c.start()

    def remote(src, dst, send, recv, seg, exp):
        return pltpu.make_async_remote_copy(
            src_ref=src, dst_ref=dst, send_sem=send, recv_sem=recv, device_id=(seg, exp), device_id_type=MESH
        )

    copies[0].wait()
    copies[1].wait()
    lane = lax.broadcasted_iota(jnp.int32, (rows, 128), 1)
    lane_e = lax.rem(lane, 32) // CAP
    lane_c = lax.rem(lane, CAP)
    tri = (
        lax.broadcasted_iota(jnp.int32, (rows, rows), 0) >= lax.broadcasted_iota(jnp.int32, (rows, rows), 1)
    ).astype(F32).astype(BF16)
    for t in range(TICKS):
        share = jnp.zeros((rows, 128), F32)
        member = jnp.zeros((rows, 128), F32)
        idt = jnp.transpose(ids_v[t])
        rwt = jnp.transpose(rw_v[t])
        for k in range(idt.shape[1]):
            hit = idt[:, k : k + 1] == lane_e
            share = share + jnp.where(hit, rwt[:, k : k + 1], F32(0.0))
            member = jnp.where(hit, F32(1.0), member)
        rank = jnp.dot(tri, member.astype(BF16), preferred_element_type=F32)
        placed = jnp.where(rank == (lane_c + 1).astype(F32), member, F32(0.0))
        place[t] = placed.astype(BF16)
        weight = placed * share
        high = weight.astype(BF16)
        low = (weight - high.astype(F32)).astype(BF16)
        zero = jnp.zeros_like(weight)
        wloc[t] = jnp.where(lane < 32, high.astype(F32), jnp.where(lane < 64, low.astype(F32), zero)).astype(BF16)

    def norm_pack(t, source):
        total = jnp.zeros((rows, 1), F32)
        for j in range(GROUP):
            v = source[:, j * cols : (j + 1) * cols].astype(F32)
            total = total + jnp.sum(v * v, axis=-1, keepdims=True)
        scale = lax.rsqrt(total / width + EPS)
        pick = place[t][:, 0:32]
        for j in range(GROUP):
            v = source[:, j * cols : (j + 1) * cols].astype(F32)
            g = gain_v[0:1, j * cols : (j + 1) * cols].astype(F32)
            normed = (v * scale * g).astype(BF16)
            rowset = lax.dot_general(pick, normed, (((0,), (0,)), ((), ())), preferred_element_type=F32)
            packed[t, :, :, j * cols : (j + 1) * cols] = rowset.astype(BF16).reshape(PAIRS, CAP, cols)

    copies[2].wait()
    copies[3].wait()
    norm_pack(0, xin)
    pl.semaphore_wait(barrier, count)

    def landing(t):
        return (xprev, wprev, ret) if t < TICKS - 1 else (x_out, w_out, r_out)

    def arrive(t):
        at, wt, rt = landing(t)
        remote(at, at, nx_send.at[t], nx_recv.at[t], nxt, p).wait_recv()
        remote(wt, wt, nw_send.at[t], nw_recv.at[t], nxt, p).wait_recv()
        remote(rt, rt, ret_send.at[t], ret_recv.at[t], nxt, p).wait_recv()

    def pair_of(c):
        return row_of(NEAR[CHUNKS[c][0]]) // 2

    def kind_of(c):
        return (0, 2 - b, 1 + b, 3)[c]

    for t in range(TICKS):
        if t > 0:
            arrive(t - 1)
            for j in range(GROUP):
                span = slice(j * cols, (j + 1) * cols)
                xcur[:, span] = combined(xprev[:, span], wprev[...], ret[:, :, span])
            norm_pack(t, xcur)

        def cell(k, column):
            row = row_of(NEAR[k])
            return rbuf.at[t, row // 2, lax.rem(row, 2) * XS + column]

        def hand(block, arrived):
            remote(block, block, y_send.at[t], arrived, s, row_of(1) * XS + x).start()

        def far_halves(k):
            far = cell(k, across)
            for side, span in ((0, (0, half)), (1, (half, width))):
                part = far.at[:, span[0] : span[1]]
                remote(part, part, xh_send.at[t], xh_recv.at[t, k, side], s, home + right).wait_recv()

        def hand_far():
            far_halves(WHOLE)
            hand(cell(WHOLE, across), xh_recv.at[t, HANDED, 0])

        def send(k):
            mine = cell(k, x)
            if k > 0:
                remote(mine, mine, y_send.at[t], y_recv.at[t * 8 + k], s, home + right).wait_recv()
            remote(mine, mine, xf_send.at[t], xf_recv.at[t, k, 0], s, home + right).start()
            remote(mine, mine, xf_send.at[t], xf_recv.at[t, k, 1], s, home + left).start()
            if NEAR[k] < 0:
                onward = NEAR.index(1 - NEAR[k])
                hand(mine, y_recv.at[t * 8 + onward])

        def relay(k):
            from_left, from_right = cell(k, left), cell(k, right)
            remote(from_left, from_left, xf_send.at[t], xf_recv.at[t, k, 0], s, home + right).wait_recv()
            part = from_left.at[:, 0:half]
            remote(part, part, xh_send.at[t], xh_recv.at[t, k, 0], s, home + right).start()
            remote(from_right, from_right, xf_send.at[t], xf_recv.at[t, k, 1], s, home + left).wait_recv()
            part = from_right.at[:, half:width]
            remote(part, part, xh_send.at[t], xh_recv.at[t, k, 1], s, home + left).start()
            if k == WHOLE:
                hand(from_left, xf_recv.at[t, HANDED, 0])
                hand(from_right, xf_recv.at[t, HANDED, 1])

        def gate_up(c):
            if t == 0 and c == 1:
                copies[4].wait()
                copies[5].wait()
            for k in CHUNKS[c]:
                if k == HANDED:
                    for column, arrived in (
                        (x, y_recv.at[t * 8 + k]),
                        (left, xf_recv.at[t, k, 0]),
                        (right, xf_recv.at[t, k, 1]),
                        (across, xh_recv.at[t, k, 0]),
                    ):
                        block = cell(k, column)
                        remote(block, block, y_send.at[t], arrived, s, row_of(1) * XS + x).wait_recv()
                elif k != WHOLE:
                    far_halves(k)
            pp = pair_of(c)
            taken = rbuf[t, pp].reshape(GROUP * CAP, width)
            both = jnp.dot(taken, wgu[...], preferred_element_type=F32)
            gate, up = both[:, 0:128], both[:, 128:256]
            act[t, q, pp] = (gate / (1.0 + jnp.exp(-gate)) * up).astype(BF16)
            mine = act.at[t, q, pp]
            for step in (1, 3, 5, 7, 4, 2, 6):
                other = lax.rem(q + step, GROUP)
                remote(
                    mine, mine, act_send.at[t], act_recv.at[t * PAIRS + kind_of(c)], s, pr * GROUP + other
                ).start()

        def resplit(other):
            remote(
                wd.at[0, :, pl.ds(pl.multiple_of(other * cols, 128), cols)], wd2.at[q],
                wd_send.at[0], wd_recv.at[0], s, pr * GROUP + other,
            ).start()

        def down(c):
            pp = lax.rem(pr + (0, 1, 3, 2)[c], PAIRS)
            kind = (0, 1, 2, 3)[c]
            block = act.at[t, 0:7, 0]
            remote(block, block, act_send.at[t], act_recv.at[t * PAIRS + kind], s, pr * GROUP).wait_recv()
            units = jnp.concatenate([act[t, k, pp] for k in range(GROUP)], axis=1)
            full = jnp.dot(units, wd2[...].reshape(GROUP * 128, cols), preferred_element_type=F32)
            outb[t, pp] = full.astype(BF16).reshape(GROUP, CAP, cols)
            for step in range(GROUP):
                owner = lax.rem(q + step, GROUP)
                remote(
                    outb.at[t, pp, owner], there_r.at[pr, :, pl.ds(pl.multiple_of(q * cols, 128), cols)],
                    ret_send.at[t], ret_recv.at[t], nxt, pp * GROUP + owner,
                ).start()

        for offset, seen in STEPS_OUT:
            target = row_of(offset)
            remote(
                packed.at[t, target // 2], rbuf.at[t, pr, q], y_send.at[t], y_recv.at[t * 8 + NEAR.index(seen)],
                s, target * XS + x,
            ).start()
        rbuf[t, pr, q] = packed[t, pr]
        there_x, there_w, there_r = landing(t)
        remote(hid.at[0] if t == 0 else xcur, there_x, nx_send.at[t], nx_recv.at[t], nxt, p).start()
        remote(wloc.at[t], there_w, nw_send.at[t], nw_recv.at[t], nxt, p).start()

        for step in PLAN[t]:
            what, arg = step[0], step[1:]
            if what == "S":
                send(int(arg))
            elif what == "R":
                relay(int(arg))
            elif what == "F":
                hand_far()
            elif what == "G":
                gate_up(int(arg))
            elif what == "D":
                down(int(arg))
            elif what == "V":
                copies[6].wait()
                remote(wd2.at[0:7], wd2.at[0:7], wd_send.at[0], wd_recv.at[0], s, pr * GROUP).wait_recv()
            else:
                column = {"+1": right, "-1": left, "2": across, "m": x, "+5": right, "-5": left, "6": across}[arg]
                resplit((b if arg in ("+1", "-1", "2") else 1 - b) * XS + column)

    arrive(TICKS - 1)
    for t in range(TICKS):
        remote(rbuf.at[t, 0:2, 0:5], rbuf.at[t, 0:2, 0:5], y_send.at[t], y_recv.at[0], s, p).wait_send()
        remote(rbuf.at[t, 0:2, 0:7], rbuf.at[t, 0:2, 0:7], xf_send.at[t], xf_recv.at[t, 0, 0], s, p).wait_send()
        remote(rbuf.at[t, 0, 0:7], rbuf.at[t, 0, 0:7], xh_send.at[t], xh_recv.at[t, 0, 0], s, p).wait_send()
        remote(act.at[t, 0:7], act.at[t, 0:7], act_send.at[t], act_recv.at[0], s, p).wait_send()
        remote(ret, ret, ret_send.at[t], ret_recv.at[t], s, p).wait_send()
        remote(xprev, xprev, nx_send.at[t], nx_recv.at[t], s, p).wait_send()
        remote(wprev, wprev, nw_send.at[t], nw_recv.at[t], s, p).wait_send()
    remote(wd2.at[0:7], wd2.at[0:7], wd_send.at[0], wd_recv.at[0], s, p).wait_send()


def body(hidden, expert_ids, route_weights, norm_gain, w_gate, w_up, w_down):
    _, rows, width = hidden.shape
    cols = width // GROUP
    top = expert_ids.shape[-1]
    dma = pltpu.SemaphoreType.DMA
    landed = pl.pallas_call(
        kernel,
        out_shape=(
            jax.ShapeDtypeStruct((rows, width), BF16),
            jax.ShapeDtypeStruct((rows, 128), BF16),
            jax.ShapeDtypeStruct((PAIRS, CAP, width), BF16),
        ),
        in_specs=[pl.BlockSpec(memory_space=pl.ANY)] * 7,
        out_specs=[pl.BlockSpec(memory_space=pl.ANY)] * 3,
        scratch_shapes=[
            pltpu.VMEM((rows, width), BF16),
            pltpu.VMEM((TICKS, top, rows), jnp.int32),
            pltpu.VMEM((TICKS, top, rows), F32),
            pltpu.VMEM((1, width), BF16),
            pltpu.VMEM((width, 256), BF16),
            pltpu.VMEM((GROUP, 128, cols), BF16),
            pltpu.VMEM((rows, width), BF16),
            pltpu.VMEM((rows, width), BF16),
            pltpu.VMEM((TICKS, rows, 128), BF16),
            pltpu.VMEM((rows, 128), BF16),
            pltpu.VMEM((TICKS, rows, 128), BF16),
            pltpu.VMEM((TICKS, PAIRS, CAP, width), BF16),
            pltpu.VMEM((TICKS, PAIRS, GROUP, CAP, width), BF16),
            pltpu.VMEM((TICKS, GROUP, PAIRS, GROUP * CAP, 128), BF16),
            pltpu.VMEM((TICKS, PAIRS, GROUP, CAP, cols), BF16),
            pltpu.VMEM((PAIRS, CAP, width), BF16),
            dma((7,)),
            dma((1,)), dma((1,)),
            dma((TICKS,)), dma((TICKS * 8,)),
            dma((TICKS,)), dma((TICKS, 8, 2)),
            dma((TICKS,)), dma((TICKS, 8, 2)),
            dma((TICKS,)), dma((TICKS * PAIRS,)),
            dma((TICKS,)), dma((TICKS,)),
            dma((TICKS,)), dma((TICKS,)),
            dma((TICKS,)), dma((TICKS,)),
        ],
        compiler_params=pltpu.CompilerParams(collective_id=0, has_side_effects=True),
    )(hidden, jnp.swapaxes(expert_ids, 2, 3), jnp.swapaxes(route_weights, 2, 3), norm_gain, w_gate, w_up, w_down)
    part = width // 2
    return pl.pallas_call(
        finish,
        grid=(2,),
        out_shape=jax.ShapeDtypeStruct(hidden.shape, BF16),
        in_specs=[
            pl.BlockSpec((rows, part), lambda i: (0, i)),
            pl.BlockSpec((rows, 128), lambda i: (0, 0)),
            pl.BlockSpec((PAIRS, CAP, part), lambda i: (0, 0, i)),
        ],
        out_specs=pl.BlockSpec((1, rows, part), lambda i: (0, 0, i)),
    )(*landed)


def solution(mesh):
    return jax.shard_map(
        body,
        mesh=mesh,
        in_specs=(
            P("segment", "expert", None),
            P(None, "segment", "expert", None),
            P(None, "segment", "expert", None),
            P("segment", None),
            P("segment", None, "expert"),
            P("segment", None, "expert"),
            P("segment", "expert", None),
        ),
        out_specs=P("segment", "expert", None),
        check_vma=False,
    )
```
